32 devices in a mesh: dp: 4 (over y, core), seq: 8 (over z, x).
Axes of the slice: x: 2, y: 2, z: 4, core: 2. Of those that a mesh axis runs over, the one named last changes fastest.
Arguments:
- queries: bfloat16 [12288, 14, 128], P(('dp', 'seq')), parts along dimension 0, may hold values from -24 to 24
- key_heads: bfloat16 [12288, 2, 128], P(('dp', 'seq')), parts along dimension 0, may hold values from -24 to 24
- value_heads: bfloat16 [12288, 2, 128], P(('dp', 'seq')), parts along dimension 0, may hold values from -6 to 6
- output_grad: bfloat16 [12288, 14, 128], P(('dp', 'seq')), parts along dimension 0, may hold values from -24 to 24
- window: int32 [96], P(('dp', 'seq')), parts along dimension 0, may hold values from 1 to 4
- retrieved: int32 [96, 4], P(('dp', 'seq')), parts along dimension 0, may hold values from 0 to 21, as said below
Outputs:
- query_grad: bfloat16 [12288, 14, 128], P(('dp', 'seq')), parts along dimension 0
- key_grad: bfloat16 [12288, 2, 128], P(('dp', 'seq')), parts along dimension 0
- value_grad: bfloat16 [12288, 2, 128], P(('dp', 'seq')), parts along dimension 0
The draws below stay inside these ranges and needn't reach their ends.
There are 4 independent parts, one for each index of `dp`. The reference program is written for one: setup_inputs(seed, part) draws one part's arguments, and reference() takes and returns one part's arrays. A program takes and returns all parts, laid end to end along the dimension named above; each array names one. Nothing has to cross between parts.
Inputs may be any that keep to these rules, and one draw needn't show every extreme that they name: retrieved[i, r] is at most i. The entries of the 3 query blocks g * 3 to g * 3 + 2 name at most one distinct block among the blocks d * 3 to d * 3 + 2, for every g and d.
All inputs are finite; a program needn't handle non-finite values.
Results may differ from the reference program's by a relative error of at most 0.0075.
Values may be sent and summed in bfloat16 or wider, within the bound.
No kernel may reach another device: no remote copies, remote signals or barrier semaphores. Data moves between devices by JAX's collectives and lax.ppermute only.
A program may use at most 128 MiB of HBM per device.

```python
import jax
import jax.numpy as jnp
from jax import lax

HD = 128
QH = 14
KVH = 2
BLOCK = 128
MEMORY = 4
BPD = 3
WINDOW_MAX = 4
SEQLEN = 3072
NBLK = 24
N_SEQ = 8


def draw_queries(key, part):
    base = jax.random.truncated_normal(jax.random.fold_in(key, 101), -6.0, 6.0, (SEQLEN, QH, HD), jnp.float32)
    return base.astype(jnp.bfloat16)


def draw_key_heads(key, part):
    base = jax.random.truncated_normal(jax.random.fold_in(key, 201), -6.0, 6.0, (SEQLEN, KVH, HD), jnp.float32)
    return base.astype(jnp.bfloat16)


def draw_window(key, part):
    widths = jax.random.randint(jax.random.fold_in(key, 11), (NBLK,), 1, WINDOW_MAX + 1, jnp.int32)
    widest = jax.random.randint(jax.random.fold_in(key, 12), (), 0, NBLK, jnp.int32)
    return widths.at[widest].set(WINDOW_MAX).astype(jnp.int32)


def draw_retrieved(key, part):
    owners = NBLK // BPD
    blocks = jnp.arange(NBLK, dtype=jnp.int32)
    device_of = blocks // BPD
    hot_offset = jax.random.randint(jax.random.fold_in(key, 41), (owners, owners), 0, BPD, jnp.int32)
    first_draw = jax.random.randint(jax.random.fold_in(key, 42), (NBLK, MEMORY), 0, 1024, jnp.int32)
    second_draw = jax.random.randint(jax.random.fold_in(key, 43), (NBLK, MEMORY), 0, 1024, jnp.int32)
    owner_device = (device_of[:, None] + 1) * first_draw * second_draw // 1048576
    owner_device = jnp.minimum(owner_device, owners - 1).astype(jnp.int32)
    requester = jnp.broadcast_to(device_of[:, None], (NBLK, MEMORY))
    picked = hot_offset[requester, owner_device]
    chosen_block = jnp.where(owner_device < device_of[:, None], owner_device * BPD + picked, device_of[:, None] * BPD)
    chosen_block = chosen_block.at[NBLK - 1, 0].set((owners - 1) * BPD)
    return chosen_block.astype(jnp.int32)


def block_scale(own_key, dims, shards, low, largest):
    def one(dim, shards_of):
        heights = jax.random.uniform(jax.random.fold_in(jax.random.fold_in(own_key, 6), dim), (shards_of,), jnp.float32, low / len(shards), largest / len(shards))
        return jnp.repeat(jnp.exp(heights), dims[dim] // shards_of).reshape((-1,) + (1,) * (len(dims) - dim - 1))

    gain = one(*shards[0])
    for cut in shards[1:]:
        gain = gain * one(*cut)
    return gain


def normal_values(stream_key, extent, scale, most, shards=(), kind=jnp.bfloat16):
    level = block_scale(stream_key, extent, shards, -0.22, 0.18) if shards else 1.0
    values = jax.random.normal(stream_key, extent, jnp.float32) * scale * level
    return jnp.minimum(jnp.maximum(values, -most), most).astype(kind)


def setup_inputs(seed: int = 0, part: int = 0) -> dict:
    streams_of = jax.random.split(jax.random.key(seed), 7)
    own_keys = jax.random.split(jax.random.fold_in(streams_of[6], part), 7)
    queries = draw_queries(jax.random.fold_in(jax.random.fold_in(streams_of[6], part), 71), part)
    key_heads = draw_key_heads(jax.random.fold_in(jax.random.fold_in(streams_of[6], part), 71), part)
    value_heads = normal_values(own_keys[2], (SEQLEN, KVH, HD), 1.0, 6.0, ((0, 8),))
    output_grad = normal_values(own_keys[3], (SEQLEN, QH, HD), 4.0, 24.0, ((0, 8),))
    window = draw_window(jax.random.fold_in(jax.random.fold_in(streams_of[6], part), 71), part)
    retrieved = draw_retrieved(jax.random.fold_in(jax.random.fold_in(streams_of[6], part), 71), part)
    return {"queries": queries, "key_heads": key_heads, "value_heads": value_heads, "output_grad": output_grad, "window": window, "retrieved": retrieved}


masked_score = -1e30


def attend(query_block, grad_block, key_rows, value_rows, allowed, score_scale):
    query_wide = query_block.astype(jnp.float32)
    grad_wide = grad_block.astype(jnp.float32)
    key_wide = key_rows.astype(jnp.float32)
    value_wide = value_rows.astype(jnp.float32)
    scores = jnp.einsum("qhgd,khd->hgqk", query_wide, key_wide) * score_scale
    scores = jnp.where(allowed[None, None], scores, masked_score)
    row_max = jnp.max(scores, axis=-1, keepdims=True)
    weights = jnp.where(allowed[None, None], jnp.exp(scores - row_max), 0.0)
    row_total = jnp.sum(weights, axis=-1, keepdims=True)
    probs = weights / row_total
    probs_half = probs.astype(jnp.bfloat16).astype(jnp.float32)
    outputs = jnp.einsum("hgqk,khd->qhgd", probs_half, value_wide)
    delta = jnp.moveaxis(jnp.sum(grad_wide * outputs, axis=-1), 0, -1)
    grad_probs = jnp.einsum("qhgd,khd->hgqk", grad_wide, value_wide)
    grad_scores = (probs * (grad_probs - delta[..., None])).astype(jnp.bfloat16).astype(jnp.float32)
    query_grad = jnp.einsum("hgqk,khd->qhgd", grad_scores, key_wide) * score_scale
    key_grad = jnp.einsum("hgqk,qhgd->khd", grad_scores, query_wide) * score_scale
    value_grad = jnp.einsum("hgqk,qhgd->khd", probs_half, grad_wide)
    return query_grad, key_grad, value_grad


def reference(queries, key_heads, value_heads, output_grad, window, retrieved):
    group_size = QH // KVH
    score_scale = HD ** -0.5
    near_count = WINDOW_MAX
    cand_count = near_count + MEMORY
    key_value = jnp.stack([key_heads, value_heads]).reshape(2, NBLK, BLOCK, KVH, HD)
    padded = jnp.concatenate([jnp.zeros((2, near_count - 1, BLOCK, KVH, HD), key_value.dtype), key_value], axis=1)
    query_blocks = queries.reshape(NBLK, BLOCK, KVH, group_size, HD)
    grad_blocks = output_grad.reshape(NBLK, BLOCK, KVH, group_size, HD)
    near_offsets = jnp.arange(near_count, dtype=jnp.int32)
    key_index = jnp.arange(cand_count * BLOCK, dtype=jnp.int32)
    query_index = jnp.arange(BLOCK, dtype=jnp.int32)
    causal = (key_index[None, :] // BLOCK != near_count - 1) | (key_index[None, :] % BLOCK <= query_index[:, None])
    earlier_entry = jnp.arange(MEMORY)[None, :] < jnp.arange(MEMORY)[:, None]

    def per_block(block_row):
        earliest = block_row - window[block_row]
        near_blocks = block_row - near_count + 1 + near_offsets
        near_live = (near_blocks >= 0) & (near_blocks > earliest)
        memory_rows = retrieved[block_row]
        repeated = jnp.any((memory_rows[:, None] == memory_rows[None, :]) & earlier_entry, axis=1)
        far_live = (memory_rows <= earliest) & jnp.logical_not(repeated)
        block_live = jnp.concatenate([near_live, far_live])
        allowed = jnp.repeat(block_live, BLOCK)[None, :] & causal
        near_pair = lax.dynamic_slice_in_dim(padded, block_row, near_count, axis=1)
        far_pair = jnp.take(key_value, memory_rows, axis=1)
        candidates = jnp.concatenate([near_pair, far_pair], axis=1).reshape(2, cand_count * BLOCK, KVH, HD)
        query_grad, key_grad, value_grad = attend(query_blocks[block_row], grad_blocks[block_row], candidates[0], candidates[1], allowed, score_scale)
        grads = jnp.stack([key_grad, value_grad]).reshape(2, cand_count, BLOCK, KVH, HD)
        return query_grad.reshape(BLOCK, QH, HD).astype(jnp.bfloat16), grads[:, :near_count], jnp.moveaxis(grads[:, near_count:], 1, 0)

    query_grads, near_grads, far_grads = lax.map(per_block, jnp.arange(NBLK, dtype=jnp.int32))
    near_total = jnp.zeros((2, NBLK + near_count - 1, BLOCK, KVH, HD), jnp.float32)
    for offset in range(near_count):
        near_total = near_total.at[:, offset:offset + NBLK].add(jnp.moveaxis(near_grads[:, :, offset], 0, 1))
    near_total = near_total[:, near_count - 1:]
    far_flat = far_grads.reshape(N_SEQ, BPD * MEMORY, 2, BLOCK, KVH, HD)
    row_flat = retrieved.reshape(N_SEQ, BPD * MEMORY)

    def per_group(summed, item):
        entries, entry_rows = item
        partial_sum = jnp.zeros((NBLK, 2, BLOCK, KVH, HD), jnp.float32).at[entry_rows].add(entries)
        rounded = lax.optimization_barrier(partial_sum.astype(jnp.bfloat16)).astype(jnp.float32)
        return summed + rounded, None

    far_total, unused = lax.scan(per_group, jnp.zeros((NBLK, 2, BLOCK, KVH, HD), jnp.float32), (far_flat, row_flat))
    summed = near_total + jnp.moveaxis(far_total, 0, 1)
    key_grad = summed[0].reshape(SEQLEN, KVH, HD).astype(jnp.bfloat16)
    value_grad = summed[1].reshape(SEQLEN, KVH, HD).astype(jnp.bfloat16)
    return query_grads.reshape(SEQLEN, QH, HD), key_grad, value_grad
```

```python
import functools
import math

import jax
import jax.numpy as jnp
from jax import lax
from jax.experimental import pallas as pl
from jax.experimental.pallas import tpu as pltpu
from jax.sharding import PartitionSpec as P

HD = 128
QH = 14
KVH = 2
GROUP = QH // KVH
BLOCK = 128
MEMORY = 4
PAD = 16
ROWS = GROUP * BLOCK
SCALE = HD ** (-0.5)
LOG2E = math.log2(math.e)

masked_score = -1e30


def shifted(array, axis, by):
    length = lax.axis_size(axis)
    pairs = [(i, i + by) for i in range(length) if 0 <= i + by < length]
    return lax.ppermute(array, axis, pairs)


def contract(a, b, dims):
    return lax.dot_general(a, b, (dims, ((), ())), preferred_element_type=jnp.float32)


def kernel(per_device, shards, own_ref, win_ref, ret_ref, q_ref, g_ref, prev_ref, kv_ref, far_ref,
           dq_ref, dprev_ref, down_ref, dfar_ref,
           wide, wide_out, qh, gh, kvs, acc, s_ref, dp_ref, dqt, slots):
    b = pl.program_id(0)
    near = 2 * per_device

    @pl.when(b == 0)
    def _():
        acc[...] = jnp.zeros_like(acc)
        kvs[0:per_device] = prev_ref[...]
        kvs[per_device:near] = kv_ref[...]
        kvs[near:near + shards] = far_ref[...]

    i = own_ref[0] * per_device + b
    earliest = i - win_ref[b]
    slots[0] = b + per_device
    count = jnp.int32(1)
    for t in range(per_device):
        j = i - per_device + t
        slots[count] = b + t
        count = count + ((j >= 0) & (j > earliest)).astype(jnp.int32)
    for r in range(MEMORY):
        e = ret_ref[b, r]
        live = e <= earliest
        for r2 in range(r):
            live = live & (e != ret_ref[b, r2])
        slots[count] = near + e // per_device
        count = count + live.astype(jnp.int32)

    flat = wide.reshape(BLOCK * PAD, HD)
    for src, dst in ((q_ref, qh), (g_ref, gh)):
        wide[:, :QH, :] = src[...].astype(jnp.float32)
        for h in range(QH):
            dst[h * BLOCK:(h + 1) * BLOCK, :] = flat[pl.ds(h, BLOCK, stride=PAD), :].astype(jnp.bfloat16)

    key_pos = lax.broadcasted_iota(jnp.int32, (BLOCK, ROWS), 0)
    query_pos = lax.broadcasted_iota(jnp.int32, (BLOCK, ROWS), 1) % BLOCK
    flat_out = wide_out.reshape(BLOCK * PAD, HD)

    def fold(x, op):
        r = x[0:8]
        for k in range(1, BLOCK // 8):
            r = op(r, x[8 * k:8 * k + 8])
        return r

    for h in range(KVH):
        head = pl.ds(h * ROWS, ROWS)

        def rows_of(n):
            return pl.ds(pl.multiple_of(n * BLOCK, BLOCK), BLOCK)

        def first(n, top):
            c = slots[n]
            s = contract(kvs[c, 0, h], qh[head, :], ((1,), (1,)))
            dp_ref[rows_of(n), :] = contract(kvs[c, 1, h], gh[head, :], ((1,), (1,)))
            return s, top

        def score(n, top):
            s, top = first(n, top)
            s_ref[rows_of(n), :] = s
            return jnp.maximum(top, fold(s, jnp.maximum))

        s, _ = first(0, None)
        s = jnp.where(key_pos <= query_pos, s, masked_score)
        s_ref[rows_of(0), :] = s
        top = lax.fori_loop(1, count, score, fold(s, jnp.maximum))
        top = jnp.max(top, axis=0, keepdims=True)

        def weigh(n, total):
            e = jnp.exp2((s_ref[rows_of(n), :] - top) * (SCALE * LOG2E))
            s_ref[rows_of(n), :] = e
            return total + fold(e, jnp.add)

        total = lax.fori_loop(0, count, weigh, jnp.zeros((8, ROWS), jnp.float32))
        inverse = 1.0 / jnp.sum(total, axis=0, keepdims=True)

        def weigh_grad(n, delta):
            p = (s_ref[rows_of(n), :] * inverse).astype(jnp.bfloat16).astype(jnp.float32)
            return delta + fold(p * dp_ref[rows_of(n), :], jnp.add)

        delta = lax.fori_loop(0, count, weigh_grad, jnp.zeros((8, ROWS), jnp.float32))
        delta = jnp.sum(delta, axis=0, keepdims=True)

        dqt[...] = jnp.zeros_like(dqt)

        def grads(n, carry):
            c = slots[n]
            p = s_ref[rows_of(n), :] * inverse
            ds = (p * (dp_ref[rows_of(n), :] - delta)).astype(jnp.bfloat16)
            acc[c, 1, h] += contract(p.astype(jnp.bfloat16), gh[head, :], ((1,), (0,)))
            acc[c, 0, h] += contract(ds, qh[head, :], ((1,), (0,)))
            dqt[...] += contract(kvs[c, 0, h], ds, ((0,), (0,)))
            return carry

        lax.fori_loop(0, count, grads, 0)
        for g in range(GROUP):
            piece = dqt[:, g * BLOCK:(g + 1) * BLOCK] * SCALE
            flat_out[pl.ds(h * GROUP + g, BLOCK, stride=PAD), :] = piece.T
    dq_ref[...] = wide_out[:, :QH, :].astype(jnp.bfloat16)

    @pl.when(b == per_device - 1)
    def _():
        for k in range(2):
            factor = SCALE if k == 0 else 1.0
            dprev_ref[:, k] = (acc[0:per_device, k] * factor).astype(jnp.bfloat16)
            down_ref[:, k] = acc[per_device:near, k] * factor
            dfar_ref[:, k] = (acc[near:near + shards, k] * factor).astype(jnp.bfloat16)


def attention_grads(own, window, retrieved, queries, output_grad, prev, kv, far):
    per_device = kv.shape[0]
    shards = far.shape[0]
    total = 2 * per_device + shards
    most = per_device + 1 + MEMORY

    def whole(shape):
        return pl.BlockSpec(shape, lambda b: (0,) * len(shape))

    smem = pl.BlockSpec(memory_space=pltpu.SMEM)
    tokens = pl.BlockSpec((BLOCK, QH, HD), lambda b: (b, 0, 0))
    half = (2, KVH, BLOCK, HD)
    return pl.pallas_call(
        functools.partial(kernel, per_device, shards),
        grid=(per_device,),
        in_specs=[smem, smem, smem, tokens, tokens, whole((per_device, *half)),
                  whole((per_device, *half)), whole((shards, *half))],
        out_specs=[tokens, whole((per_device, *half)), whole((per_device, *half)), whole((shards, *half))],
        out_shape=[
            jax.ShapeDtypeStruct(queries.shape, jnp.bfloat16),
            jax.ShapeDtypeStruct((per_device, *half), jnp.bfloat16),
            jax.ShapeDtypeStruct((per_device, *half), jnp.float32),
            jax.ShapeDtypeStruct((shards, *half), jnp.bfloat16),
        ],
        scratch_shapes=[
            pltpu.VMEM((BLOCK, PAD, HD), jnp.float32),
            pltpu.VMEM((BLOCK, PAD, HD), jnp.float32),
            pltpu.VMEM((QH * BLOCK, HD), jnp.bfloat16),
            pltpu.VMEM((QH * BLOCK, HD), jnp.bfloat16),
            pltpu.VMEM((total, *half), jnp.bfloat16),
            pltpu.VMEM((total, *half), jnp.float32),
            pltpu.VMEM((most * BLOCK, ROWS), jnp.float32),
            pltpu.VMEM((most * BLOCK, ROWS), jnp.float32),
            pltpu.VMEM((HD, ROWS), jnp.float32),
            pltpu.SMEM((most + 1,), jnp.int32),
        ],
        name="attention_grads",
    )(own, window, retrieved, queries, output_grad, prev, kv, far)


def body(queries, key_heads, value_heads, output_grad, window, retrieved):
    tokens = queries.shape[0]
    per_device = tokens // BLOCK
    shards = lax.axis_size("seq")
    own_index = lax.axis_index("seq").astype(jnp.int32)
    named = retrieved.reshape(1, per_device * MEMORY)
    owners = jnp.arange(shards, dtype=jnp.int32)[:, None]
    wants = jnp.max(jnp.where(named // per_device == owners, named % per_device, -1), axis=1)
    wanted = lax.all_to_all(wants, "seq", split_axis=0, concat_axis=0, tiled=True)

    kv = jnp.stack([key_heads, value_heads]).reshape(2, per_device, BLOCK, KVH, HD)
    kv = kv.transpose(1, 0, 3, 2, 4)
    prev = shifted(kv, "seq", 1)
    outgoing = jnp.take(kv, jnp.maximum(wanted, 0), axis=0)
    far = lax.all_to_all(outgoing, "seq", split_axis=0, concat_axis=0, tiled=True)
    query_grad, dprev, down, dfar = attention_grads(
        own_index.reshape(1), window, retrieved, queries, output_grad, prev, kv, far
    )
    replies = lax.all_to_all(dfar, "seq", split_axis=0, concat_axis=0, tiled=True)
    returned = shifted(dprev, "seq", -1).astype(jnp.float32)
    slot_hits = (wanted[:, None] == jnp.arange(per_device)[None, :]).astype(jnp.bfloat16)
    far_sum = jnp.einsum("eb,e...->b...", slot_hits, replies, preferred_element_type=jnp.float32)
    summed = (down + returned + far_sum).transpose(1, 0, 3, 2, 4).astype(jnp.bfloat16)
    summed = summed.reshape(2, tokens, KVH, HD)
    return query_grad, summed[0], summed[1]


def solution(mesh):
    rows = P(("dp", "seq"), None, None)
    return jax.shard_map(
        body,
        mesh=mesh,
        in_specs=(rows, rows, rows, rows, P(("dp", "seq")), P(("dp", "seq"), None)),
        out_specs=(rows, rows, rows),
        check_vma=False,
    )
```

```python
import functools
import math

import jax
import jax.numpy as jnp
from jax import lax
from jax.experimental import pallas as pl
from jax.experimental.pallas import tpu as pltpu
from jax.sharding import PartitionSpec as P


HD = 128
QH = 14
KVH = 2
GROUP = QH // KVH
BLOCK = 128
SLAB = 16
MEMORY = 4
ROWS = GROUP * BLOCK
SCALE = HD ** (-0.5)
LOG2E = math.log2(math.e)

masked_score = -1e30


def contract(a, b, dims):
    return lax.dot_general(a, b, (dims, ((), ())), preferred_element_type=jnp.float32)


def fold(x, op):
    r = x[0:8]
    for k in range(1, x.shape[0] // 8):
        r = op(r, x[8 * k:8 * k + 8])
    return r


def list_near(per_device, b, own_ref, win_ref, slots):
    i = own_ref[0] * per_device + b
    earliest = i - win_ref[b]
    slots[0] = b + per_device
    count = jnp.int32(1)
    for back in range(1, per_device + 1):
        j = i - back
        slots[count] = b + per_device - back
        count = count + ((j >= 0) & (j > earliest)).astype(jnp.int32)
    return earliest, count


def list_far(per_device, b, ret_ref, earliest, count, slots):
    for r in range(MEMORY):
        e = ret_ref[b, r]
        live = e <= earliest
        for r2 in range(r):
            live = live & (e != ret_ref[b, r2])
        slots[count] = 2 * per_device + e // per_device
        count = count + live.astype(jnp.int32)
    return count


def weigh(s, top):
    return jnp.exp2((s - top) * (SCALE * LOG2E))


def kernel(per_device, shards, h, own_ref, win_ref, ret_ref, q_ref, g_ref, prev_ref, kv_ref, far_ref, *refs):
    if h > 0:
        refs = refs[2:]
    dq_ref, down_ref, dprev_ref, dfar_ref, kvs, acc, s_ref, dp_ref, dqt, slots = refs
    b = pl.program_id(0)
    near = 2 * per_device

    @pl.when(b == 0)
    def _():
        acc[...] = jnp.zeros_like(acc)
        kvs[0:per_device] = prev_ref[0]
        kvs[per_device:near] = kv_ref[0]
        kvs[near:near + shards] = far_ref[...]

    earliest, count = list_near(per_device, b, own_ref, win_ref, slots)
    count = list_far(per_device, b, ret_ref, earliest, count, slots)
    qh = q_ref.reshape(ROWS, HD)
    gh = g_ref.reshape(ROWS, HD)

    def each(body, first, stop, carry, width=2):
        whole = (stop - first) // width

        def wide(m, c):
            return body(first + m * width, width, c)

        carry = lax.fori_loop(0, whole, wide, carry)
        return lax.fori_loop(first + whole * width, stop, lambda n, c: body(n, 1, c), carry)

    def rows_at(n, width):
        return pl.ds(pl.multiple_of(n * BLOCK, BLOCK), width * BLOCK)

    def blocks(n, width, which):
        return jnp.concatenate([kvs[slots[n + k], which] for k in range(width)], axis=0)

    def products(n, width):
        dp_ref[rows_at(n, width), :] = contract(blocks(n, width, 1), gh[...], ((1,), (1,)))
        return contract(blocks(n, width, 0), qh[...], ((1,), (1,)))

    def score(n, width, top):
        s = products(n, width)
        s_ref[rows_at(n, width), :] = s
        return jnp.maximum(top, fold(s, jnp.maximum))

    key_pos = lax.broadcasted_iota(jnp.int32, (BLOCK, ROWS), 0)
    query_pos = lax.broadcasted_iota(jnp.int32, (BLOCK, ROWS), 1) % BLOCK
    s = jnp.where(key_pos <= query_pos, products(0, 1), masked_score)
    s_ref[rows_at(0, 1), :] = s
    top = each(score, 1, count, fold(s, jnp.maximum))
    top = jnp.max(top, axis=0, keepdims=True)

    def slab(n, k):
        return pl.ds(pl.multiple_of(n * BLOCK, BLOCK) + k * SLAB, SLAB)

    def weigh_one(n, total):
        e = weigh(s_ref[rows_at(n, 1), :], top)
        s_ref[rows_at(n, 1), :] = e
        return total + fold(e, jnp.add)

    total = lax.fori_loop(0, count, weigh_one, jnp.zeros((8, ROWS), jnp.float32))
    inverse = 1.0 / jnp.sum(total, axis=0, keepdims=True)

    def weigh_grad(n, delta):
        for k in range(BLOCK // SLAB):
            p = (s_ref[slab(n, k), :] * inverse).astype(jnp.bfloat16).astype(jnp.float32)
            delta = delta + fold(p * dp_ref[slab(n, k), :], jnp.add)
        return delta

    delta = lax.fori_loop(0, count, weigh_grad, jnp.zeros((8, ROWS), jnp.float32))
    delta = jnp.sum(delta, axis=0, keepdims=True)
    dqt[...] = jnp.zeros_like(dqt)

    def grads(n, width, carry):
        p = s_ref[rows_at(n, width), :] * inverse
        ds = (p * (dp_ref[rows_at(n, width), :] - delta)).astype(jnp.bfloat16)
        value_terms = contract(p.astype(jnp.bfloat16), gh[...], ((1,), (0,)))
        key_terms = contract(ds, qh[...], ((1,), (0,)))
        for k in range(width):
            c = slots[n + k]
            acc[c, 1] += value_terms[k * BLOCK:(k + 1) * BLOCK]
            acc[c, 0] += key_terms[k * BLOCK:(k + 1) * BLOCK]
        dqt[...] += contract(blocks(n, width, 0), ds, ((0,), (0,)))
        return carry

    each(grads, 0, count, 0)
    for g in range(GROUP):
        piece = dqt[:, g * BLOCK:(g + 1) * BLOCK] * SCALE
        dq_ref[g] = piece.T.astype(jnp.bfloat16)

    @pl.when(b == per_device - 1)
    def _():
        for k in range(2):
            factor = SCALE if k == 0 else 1.0
            dprev_ref[:, k] = (acc[0:per_device, k] * factor).astype(jnp.bfloat16)
            down_ref[0, :, k] = acc[per_device:near, k] * factor
            dfar_ref[:, k] = (acc[near:near + shards, k] * factor).astype(jnp.bfloat16)


def attention_grads(h, own, window, retrieved, queries, output_grad, prev, kv, far, *carried):
    per_device = kv.shape[1]
    shards = far.shape[0]
    total = 2 * per_device + shards
    most = per_device + 1 + MEMORY
    pair = (2, BLOCK, HD)
    smem = pl.BlockSpec(memory_space=pltpu.SMEM)
    tokens = pl.BlockSpec((GROUP, BLOCK, HD), lambda b: (h, b, 0))
    of_head = pl.BlockSpec((1, per_device, *pair), lambda b: (h, 0, 0, 0, 0))
    of_owner = pl.BlockSpec((shards, *pair), lambda b: (0, 0, 0, 0))
    return pl.pallas_call(
        functools.partial(kernel, per_device, shards, h),
        grid=(per_device,),
        in_specs=[smem, smem, smem, tokens, tokens, of_head, of_head, of_owner]
        + [pl.BlockSpec(memory_space=pl.ANY)] * len(carried),
        out_specs=[tokens, of_head, pl.BlockSpec((per_device, *pair), lambda b: (0, 0, 0, 0)), of_owner],
        out_shape=[
            jax.ShapeDtypeStruct(queries.shape, jnp.bfloat16),
            jax.ShapeDtypeStruct((KVH, per_device, *pair), jnp.float32),
            jax.ShapeDtypeStruct((per_device, *pair), jnp.bfloat16),
            jax.ShapeDtypeStruct((shards, *pair), jnp.bfloat16),
        ],
        scratch_shapes=[
            pltpu.VMEM((total, *pair), jnp.bfloat16),
            pltpu.VMEM((total, *pair), jnp.float32),
            pltpu.VMEM((most * BLOCK, ROWS), jnp.float32),
            pltpu.VMEM((most * BLOCK, ROWS), jnp.float32),
            pltpu.VMEM((HD, ROWS), jnp.float32),
            pltpu.SMEM((most + 1,), jnp.int32),
        ],
        input_output_aliases={8: 0, 9: 1} if carried else {},
        cost_estimate=pl.CostEstimate(
            flops=10 * per_device * most * BLOCK * ROWS * HD,
            transcendentals=per_device * most * BLOCK * ROWS,
            bytes_accessed=8 * queries.size,
        ),
    )(own, window, retrieved, queries, output_grad, prev, kv, far, *carried)


def exchange(array):
    return lax.all_to_all(array, "seq", split_axis=0, concat_axis=0, tiled=True)


def shifted(array, by):
    length = lax.axis_size("seq")
    pairs = [(i, i + by) for i in range(length) if 0 <= i + by < length]
    return lax.ppermute(array, "seq", pairs)


def body(queries, key_heads, value_heads, output_grad, window, retrieved):
    tokens = queries.shape[0]
    per_device = tokens // BLOCK
    shards = lax.axis_size("seq")
    own_index = lax.axis_index("seq").astype(jnp.int32).reshape(1)
    named = retrieved.reshape(1, per_device * MEMORY)
    owners = jnp.arange(shards, dtype=jnp.int32)[:, None]
    wants = jnp.max(jnp.where(named // per_device == owners, named % per_device, -1), axis=1)
    wanted = exchange(wants)

    kv = jnp.stack([key_heads, value_heads]).reshape(2, per_device, BLOCK, KVH, HD)
    kv = kv.transpose(3, 1, 0, 2, 4)
    prev = shifted(kv, 1)
    slot_hits = (wanted[:, None] == jnp.arange(per_device)[None, :]).astype(jnp.bfloat16)
    queries = queries.transpose(1, 0, 2)
    output_grad = output_grad.transpose(1, 0, 2)
    carried = ()
    fars = []
    replies = []
    returned = []
    for h in range(KVH):
        outgoing = jnp.take(kv[h], jnp.maximum(wanted, 0), axis=0, mode="clip")
        fars.append(exchange(outgoing))
    for h in range(KVH):
        *carried, dprev, dfar = attention_grads(
            h, own_index, window, retrieved, queries, output_grad, prev, kv, fars[h], *carried
        )
        replies.append(exchange(dfar))
        returned.append(shifted(dprev, -1).astype(jnp.float32))
    query_grad, down = carried
    sums = []
    for h in range(KVH):
        far_sum = jnp.einsum(
            "eb,e...->b...", slot_hits, replies[h], preferred_element_type=jnp.float32
        )
        sums.append(down[h] + returned[h] + far_sum)
    summed = jnp.stack(sums).transpose(2, 1, 3, 0, 4).astype(jnp.bfloat16)
    summed = summed.reshape(2, tokens, KVH, HD)
    return query_grad.transpose(1, 0, 2), summed[0], summed[1]


def solution(mesh):
    rows = P(("dp", "seq"), None, None)
    return jax.shard_map(
        body,
        mesh=mesh,
        in_specs=(rows, rows, rows, rows, P(("dp", "seq")), P(("dp", "seq"), None)),
        out_specs=(rows, rows, rows),
        check_vma=False,
    )
```

```python
import functools
import math

import jax
import jax.numpy as jnp
from jax import lax
from jax.experimental import pallas as pl
from jax.experimental.pallas import tpu as pltpu
from jax.sharding import PartitionSpec as P


HD = 128
QH = 14
KVH = 2
GROUP = QH // KVH
BLOCK = 128
SLAB = 16
MEMORY = 4
ROWS = GROUP * BLOCK
SCALE = HD ** (-0.5)
LOG2E = math.log2(math.e)

masked_score = -1e30


def contract(a, b, dims):
    return lax.dot_general(a, b, (dims, ((), ())), preferred_element_type=jnp.float32)


def fold(x, op):
    r = x[0:8]
    for k in range(1, x.shape[0] // 8):
        r = op(r, x[8 * k:8 * k + 8])
    return r


def list_near(per_device, b, own_ref, win_ref, slots):
    i = own_ref[0] * per_device + b
    earliest = i - win_ref[b]
    slots[0] = b + per_device
    count = jnp.int32(1)
    for back in range(1, per_device + 1):
        j = i - back
        slots[count] = b + per_device - back
        count = count + ((j >= 0) & (j > earliest)).astype(jnp.int32)
    return earliest, count


def list_far(per_device, b, ret_ref, earliest, count, slots):
    for r in range(MEMORY):
        e = ret_ref[b, r]
        live = e <= earliest
        for r2 in range(r):
            live = live & (e != ret_ref[b, r2])
        slots[count] = 2 * per_device + e // per_device
        count = count + live.astype(jnp.int32)
    return count


def kernel(per_device, shards, h, own_ref, win_ref, ret_ref, q_ref, g_ref, prev_ref, kv_ref, far_ref, *refs):
    if h > 0:
        refs = refs[2:]
    dq_ref, down_ref, dprev_ref, dfar_ref, kvs, acc, s_ref, dp_ref, dqt, slots = refs
    b = pl.program_id(0)
    near = 2 * per_device

    @pl.when(b == 0)
    def _():
        acc[...] = jnp.zeros_like(acc)
        kvs[0:per_device] = prev_ref[0]
        kvs[per_device:near] = kv_ref[0]
        kvs[near:near + shards] = far_ref[...]

    earliest, count = list_near(per_device, b, own_ref, win_ref, slots)
    count = list_far(per_device, b, ret_ref, earliest, count, slots)
    qh = q_ref.reshape(ROWS, HD)
    gh = g_ref.reshape(ROWS, HD)

    def each(body, first, stop, carry):
        for size in (4, 2, 1):
            whole = (stop - first) // size

            def wide(m, c, first=first, size=size):
                return body(first + m * size, size, c)

            carry = lax.fori_loop(0, whole, wide, carry)
            first = first + whole * size
        return carry

    def rows_at(n, width):
        return pl.ds(pl.multiple_of(n * BLOCK, BLOCK), width * BLOCK)

    def blocks(n, width, which):
        return jnp.concatenate([kvs[slots[n + k], which] for k in range(width)], axis=0)

    def products(n, width):
        dp_ref[rows_at(n, width), :] = contract(blocks(n, width, 1), gh[...], ((1,), (1,)))
        return contract(blocks(n, width, 0), qh[...], ((1,), (1,))) * (SCALE * LOG2E)

    def score(n, width, top):
        s = products(n, width)
        s_ref[rows_at(n, width), :] = s
        return jnp.maximum(top, fold(s, jnp.maximum))

    key_pos = lax.broadcasted_iota(jnp.int32, (BLOCK, ROWS), 0)
    query_pos = lax.broadcasted_iota(jnp.int32, (BLOCK, ROWS), 1) % BLOCK
    s = jnp.where(key_pos <= query_pos, products(0, 1), masked_score)
    s_ref[rows_at(0, 1), :] = s
    top = each(score, 1, count, fold(s, jnp.maximum))
    top = jnp.max(top, axis=0, keepdims=True)

    def slab(n, k):
        return pl.ds(pl.multiple_of(n * BLOCK, BLOCK) + k * SLAB, SLAB)

    def weigh_one(n, total):
        e = jnp.exp2(s_ref[rows_at(n, 1), :] - top)
        s_ref[rows_at(n, 1), :] = e
        return total + fold(e, jnp.add)

    total = lax.fori_loop(0, count, weigh_one, jnp.zeros((8, ROWS), jnp.float32))
    inverse = 1.0 / jnp.sum(total, axis=0, keepdims=True)

    def weigh_grad(n, delta):
        for k in range(BLOCK // SLAB):
            p = (s_ref[slab(n, k), :] * inverse).astype(jnp.bfloat16).astype(jnp.float32)
            delta = delta + fold(p * dp_ref[slab(n, k), :], jnp.add)
        return delta

    delta = lax.fori_loop(0, count, weigh_grad, jnp.zeros((8, ROWS), jnp.float32))
    delta = jnp.sum(delta, axis=0, keepdims=True)
    dqt[...] = jnp.zeros_like(dqt)

    def grads(n, width, carry):
        p = s_ref[rows_at(n, width), :] * inverse
        ds = (p * (dp_ref[rows_at(n, width), :] - delta)).astype(jnp.bfloat16)
        value_terms = contract(p.astype(jnp.bfloat16), gh[...], ((1,), (0,)))
        key_terms = contract(ds, qh[...], ((1,), (0,)))
        for k in range(width):
            c = slots[n + k]
            acc[c, 1] += value_terms[k * BLOCK:(k + 1) * BLOCK]
            acc[c, 0] += key_terms[k * BLOCK:(k + 1) * BLOCK]
        dqt[...] += contract(blocks(n, width, 0), ds, ((0,), (0,)))
        return carry

    each(grads, 0, count, 0)
    for g in range(GROUP):
        piece = (dqt[:, g * BLOCK:(g + 1) * BLOCK] * SCALE).astype(jnp.bfloat16)
        dq_ref[g] = piece.T

    @pl.when(b == per_device - 1)
    def _():
        for k in range(2):
            factor = SCALE if k == 0 else 1.0
            dprev_ref[:, k] = (acc[0:per_device, k] * factor).astype(jnp.bfloat16)
            down_ref[0, :, k] = acc[per_device:near, k] * factor
            dfar_ref[:, k] = (acc[near:near + shards, k] * factor).astype(jnp.bfloat16)


def attention_grads(h, own, window, retrieved, queries, output_grad, prev, kv, far, *carried):
    per_device = kv.shape[1]
    shards = far.shape[0]
    total = 2 * per_device + shards
    most = per_device + 1 + MEMORY
    pair = (2, BLOCK, HD)
    smem = pl.BlockSpec(memory_space=pltpu.SMEM)
    tokens = pl.BlockSpec((GROUP, BLOCK, HD), lambda b: (h, b, 0))
    of_head = pl.BlockSpec((1, per_device, *pair), lambda b: (h, 0, 0, 0, 0))
    of_owner = pl.BlockSpec((shards, *pair), lambda b: (0, 0, 0, 0))
    return pl.pallas_call(
        functools.partial(kernel, per_device, shards, h),
        grid=(per_device,),
        in_specs=[smem, smem, smem, tokens, tokens, of_head, of_head, of_owner]
        + [pl.BlockSpec(memory_space=pl.ANY)] * len(carried),
        out_specs=[tokens, of_head, pl.BlockSpec((per_device, *pair), lambda b: (0, 0, 0, 0)), of_owner],
        out_shape=[
            jax.ShapeDtypeStruct(queries.shape, jnp.bfloat16),
            jax.ShapeDtypeStruct((KVH, per_device, *pair), jnp.float32),
            jax.ShapeDtypeStruct((per_device, *pair), jnp.bfloat16),
            jax.ShapeDtypeStruct((shards, *pair), jnp.bfloat16),
        ],
        scratch_shapes=[
            pltpu.VMEM((total, *pair), jnp.bfloat16),
            pltpu.VMEM((total, *pair), jnp.float32),
            pltpu.VMEM((most * BLOCK, ROWS), jnp.float32),
            pltpu.VMEM((most * BLOCK, ROWS), jnp.float32),
            pltpu.VMEM((HD, ROWS), jnp.float32),
            pltpu.SMEM((most + 1,), jnp.int32),
        ],
        input_output_aliases={8: 0, 9: 1} if carried else {},
        cost_estimate=pl.CostEstimate(
            flops=10 * per_device * most * BLOCK * ROWS * HD,
            transcendentals=per_device * most * BLOCK * ROWS,
            bytes_accessed=8 * queries.size,
        ),
    )(own, window, retrieved, queries, output_grad, prev, kv, far, *carried)


def wants_kernel(per_device, ret_ref, out_ref):
    owners = lax.broadcasted_iota(jnp.int32, out_ref.shape, 0)
    wants = jnp.full(out_ref.shape, -1, jnp.int32)
    for b in range(per_device):
        for r in range(MEMORY):
            e = ret_ref[b, r]
            wants = jnp.where(owners == e // per_device, jnp.maximum(wants, e % per_device), wants)
    out_ref[...] = wants


def wants_of(retrieved, shards):
    return pl.pallas_call(
        functools.partial(wants_kernel, retrieved.shape[0]),
        in_specs=[pl.BlockSpec(memory_space=pltpu.SMEM)],
        out_shape=jax.ShapeDtypeStruct((shards, 8, HD), jnp.int32),
        name="wants",
    )(retrieved)


def exchange(array):
    return lax.all_to_all(array, "seq", split_axis=0, concat_axis=0, tiled=True)


def shifted(array, by):
    length = lax.axis_size("seq")
    pairs = [(i, i + by) for i in range(length) if 0 <= i + by < length]
    return lax.ppermute(array, "seq", pairs)


def body(queries, key_heads, value_heads, output_grad, window, retrieved):
    tokens = queries.shape[0]
    per_device = tokens // BLOCK
    shards = lax.axis_size("seq")
    own_index = lax.axis_index("seq").astype(jnp.int32).reshape(1)
    wanted = exchange(wants_of(retrieved, shards))[:, 0, 0]

    kv = jnp.stack([key_heads, value_heads]).reshape(2, per_device, BLOCK, KVH, HD)
    kv = kv.transpose(3, 1, 0, 2, 4)
    prev = shifted(kv, 1)
    slot_hits = (wanted[:, None] == jnp.arange(per_device)[None, :]).astype(jnp.bfloat16)
    queries = queries.transpose(1, 0, 2)
    output_grad = output_grad.transpose(1, 0, 2)
    carried = ()
    fars = []
    replies = []
    returned = []
    for h in range(KVH):
        outgoing = jnp.take(kv[h], jnp.maximum(wanted, 0), axis=0, mode="clip")
        fars.append(exchange(outgoing))
    for h in range(KVH):
        *carried, dprev, dfar = attention_grads(
            h, own_index, window, retrieved, queries, output_grad, prev, kv, fars[h], *carried
        )
        replies.append(exchange(dfar))
        returned.append(shifted(dprev, -1).astype(jnp.float32))
    query_grad, down = carried
    sums = []
    for h in range(KVH):
        far_sum = jnp.einsum(
            "eb,e...->b...", slot_hits, replies[h], preferred_element_type=jnp.float32
        )
        sums.append(down[h] + returned[h] + far_sum)
    summed = jnp.stack(sums).transpose(2, 1, 3, 0, 4).astype(jnp.bfloat16)
    summed = summed.reshape(2, tokens, KVH, HD)
    return query_grad.transpose(1, 0, 2), summed[0], summed[1]


def solution(mesh):
    rows = P(("dp", "seq"), None, None)
    return jax.shard_map(
        body,
        mesh=mesh,
        in_specs=(rows, rows, rows, rows, P(("dp", "seq")), P(("dp", "seq"), None)),
        out_specs=(rows, rows, rows),
        check_vma=False,
    )
```

```python
import functools
import math

import jax
import jax.numpy as jnp
from jax import lax
from jax.experimental import pallas as pl
from jax.experimental.pallas import tpu as pltpu
from jax.sharding import PartitionSpec as P


HD = 128
QH = 14
KVH = 2
GROUP = QH // KVH
BLOCK = 128
SLAB = 16
MEMORY = 4
ROWS = GROUP * BLOCK
SCALE = HD ** (-0.5)
LOG2E = math.log2(math.e)

masked_score = -1e30


def contract(a, b, dims):
    return lax.dot_general(a, b, (dims, ((), ())), preferred_element_type=jnp.float32)


def fold(x, op):
    r = x[0:8]
    for k in range(1, x.shape[0] // 8):
        r = op(r, x[8 * k:8 * k + 8])
    return r


def list_near(per_device, b, own_ref, win_ref, slots):
    i = own_ref[0] * per_device + b
    earliest = i - win_ref[b]
    slots[0] = b + per_device
    count = jnp.int32(1)
    for back in range(1, per_device + 1):
        j = i - back
        slots[count] = b + per_device - back
        count = count + ((j >= 0) & (j > earliest)).astype(jnp.int32)
    return earliest, count


def list_far(per_device, b, ret_ref, earliest, count, slots):
    for r in range(MEMORY):
        e = ret_ref[b, r]
        live = e <= earliest
        for r2 in range(r):
            live = live & (e != ret_ref[b, r2])
        slots[count] = 2 * per_device + e // per_device
        count = count + live.astype(jnp.int32)
    return count


def kernel(per_device, shards, h, own_ref, win_ref, ret_ref, q_ref, g_ref, prev_ref, kv_ref, far_ref, *refs):
    if h > 0:
        refs = refs[2:]
    dq_ref, down_ref, dprev_ref, dfar_ref, kvs, acc, s_ref, dp_ref, dqt, slots = refs
    b = pl.program_id(0)
    near = 2 * per_device

    @pl.when(b == 0)
    def _():
        acc[...] = jnp.zeros_like(acc)
        kvs[0:per_device] = prev_ref[0]
        kvs[per_device:near] = kv_ref[0]
        kvs[near:near + shards] = far_ref[...]

    earliest, count = list_near(per_device, b, own_ref, win_ref, slots)
    count = list_far(per_device, b, ret_ref, earliest, count, slots)
    qh = q_ref.reshape(ROWS, HD)
    gh = g_ref.reshape(ROWS, HD)

    def each(body, first, stop, carry):
        for size in (4, 2, 1):
            whole = (stop - first) // size

            def wide(m, c, first=first, size=size):
                return body(first + m * size, size, c)

            carry = lax.fori_loop(0, whole, wide, carry)
            first = first + whole * size
        return carry

    def rows_at(n, width):
        return pl.ds(pl.multiple_of(n * BLOCK, BLOCK), width * BLOCK)

    def blocks(n, width, which):
        return jnp.concatenate([kvs[slots[n + k], which] for k in range(width)], axis=0)

    def products(n, width):
        dp_ref[rows_at(n, width), :] = contract(blocks(n, width, 1), gh[...], ((1,), (1,)))
        return contract(blocks(n, width, 0), qh[...], ((1,), (1,))) * (SCALE * LOG2E)

    key_pos = lax.broadcasted_iota(jnp.int32, (BLOCK, BLOCK), 0)
    query_pos = lax.broadcasted_iota(jnp.int32, (BLOCK, BLOCK), 1)
    above = jnp.where(key_pos <= query_pos, 0, 1)

    def score(n, width, top):
        s = products(n, width)
        hidden = above > n
        own = jnp.concatenate(
            [jnp.where(hidden, masked_score, s[:BLOCK, g * BLOCK:(g + 1) * BLOCK]) for g in range(GROUP)], axis=1)
        s = own if width == 1 else jnp.concatenate([own, s[BLOCK:]], axis=0)
        s_ref[rows_at(n, width), :] = s
        return jnp.maximum(top, fold(s, jnp.maximum))

    top = each(score, 0, count, jnp.full((8, ROWS), masked_score, jnp.float32))
    top = jnp.max(top, axis=0, keepdims=True)

    def slab(n, k):
        return pl.ds(pl.multiple_of(n * BLOCK, BLOCK) + k * SLAB, SLAB)

    def weigh_one(n, total):
        e = jnp.exp2(s_ref[rows_at(n, 1), :] - top)
        s_ref[rows_at(n, 1), :] = e
        return total + fold(e, jnp.add)

    total = lax.fori_loop(0, count, weigh_one, jnp.zeros((8, ROWS), jnp.float32))
    inverse = 1.0 / jnp.sum(total, axis=0, keepdims=True)

    def weigh_grad(n, delta):
        for k in range(BLOCK // SLAB):
            p = (s_ref[slab(n, k), :] * inverse).astype(jnp.bfloat16).astype(jnp.float32)
            delta = delta + fold(p * dp_ref[slab(n, k), :], jnp.add)
        return delta

    delta = lax.fori_loop(0, count, weigh_grad, jnp.zeros((8, ROWS), jnp.float32))
    delta = jnp.sum(delta, axis=0, keepdims=True)
    dqt[...] = jnp.zeros_like(dqt)

    def grads(n, width, carry):
        p = s_ref[rows_at(n, width), :] * inverse
        ds = (p * (dp_ref[rows_at(n, width), :] - delta)).astype(jnp.bfloat16)
        value_terms = contract(p.astype(jnp.bfloat16), gh[...], ((1,), (0,)))
        key_terms = contract(ds, qh[...], ((1,), (0,)))
        for k in range(width):
            c = slots[n + k]
            acc[c, 1] += value_terms[k * BLOCK:(k + 1) * BLOCK]
            acc[c, 0] += key_terms[k * BLOCK:(k + 1) * BLOCK]
        dqt[...] += contract(blocks(n, width, 0), ds, ((0,), (0,)))
        return carry

    each(grads, 0, count, 0)
    for g in range(GROUP):
        piece = (dqt[:, g * BLOCK:(g + 1) * BLOCK] * SCALE).astype(jnp.bfloat16)
        dq_ref[g] = piece.T

    @pl.when(b == per_device - 1)
    def _():
        for k in range(2):
            factor = SCALE if k == 0 else 1.0
            dprev_ref[:, k] = (acc[0:per_device, k] * factor).astype(jnp.bfloat16)
            down_ref[0, :, k] = acc[per_device:near, k] * factor
            dfar_ref[:, k] = (acc[near:near + shards, k] * factor).astype(jnp.bfloat16)


def attention_grads(h, own, window, retrieved, queries, output_grad, prev, kv, far, *carried):
    per_device = kv.shape[1]
    shards = far.shape[0]
    total = 2 * per_device + shards
    most = per_device + 1 + MEMORY
    pair = (2, BLOCK, HD)
    smem = pl.BlockSpec(memory_space=pltpu.SMEM)
    tokens = pl.BlockSpec((GROUP, BLOCK, HD), lambda b: (h, b, 0))
    of_head = pl.BlockSpec((1, per_device, *pair), lambda b: (h, 0, 0, 0, 0))
    of_owner = pl.BlockSpec((shards, *pair), lambda b: (0, 0, 0, 0))
    return pl.pallas_call(
        functools.partial(kernel, per_device, shards, h),
        grid=(per_device,),
        in_specs=[smem, smem, smem, tokens, tokens, of_head, of_head, of_owner]
        + [pl.BlockSpec(memory_space=pl.ANY)] * len(carried),
        out_specs=[tokens, of_head, pl.BlockSpec((per_device, *pair), lambda b: (0, 0, 0, 0)), of_owner],
        out_shape=[
            pltpu.HBM(queries.shape, jnp.bfloat16),
            pltpu.HBM((KVH, per_device, *pair), jnp.float32),
            pltpu.HBM((per_device, *pair), jnp.bfloat16),
            pltpu.HBM((shards, *pair), jnp.bfloat16),
        ],
        scratch_shapes=[
            pltpu.VMEM((total, *pair), jnp.bfloat16),
            pltpu.VMEM((total, *pair), jnp.float32),
            pltpu.VMEM((most * BLOCK, ROWS), jnp.float32),
            pltpu.VMEM((most * BLOCK, ROWS), jnp.float32),
            pltpu.VMEM((HD, ROWS), jnp.float32),
            pltpu.SMEM((most + 1,), jnp.int32),
        ],
        input_output_aliases={8: 0, 9: 1} if carried else {},
        cost_estimate=pl.CostEstimate(
            flops=10 * per_device * most * BLOCK * ROWS * HD,
            transcendentals=per_device * most * BLOCK * ROWS,
            bytes_accessed=8 * queries.size,
        ),
        compiler_params=pltpu.CompilerParams(vmem_limit_bytes=36 << 20),
    )(own, window, retrieved, queries, output_grad, prev, kv, far, *carried)


def wants_kernel(per_device, ret_ref, out_ref):
    owners = lax.broadcasted_iota(jnp.int32, out_ref.shape, 0)
    wants = jnp.full(out_ref.shape, -1, jnp.int32)
    for b in range(per_device):
        for r in range(MEMORY):
            e = ret_ref[b, r]
            wants = jnp.where(owners == e // per_device, jnp.maximum(wants, e % per_device), wants)
    out_ref[...] = wants


def wants_of(retrieved, shards):
    return pl.pallas_call(
        functools.partial(wants_kernel, retrieved.shape[0]),
        in_specs=[pl.BlockSpec(memory_space=pltpu.SMEM)],
        out_shape=jax.ShapeDtypeStruct((shards, 8, HD), jnp.int32),
        name="wants",
    )(retrieved)


def exchange(array):
    return lax.all_to_all(array, "seq", split_axis=0, concat_axis=0, tiled=True)


def shifted(array, by):
    length = lax.axis_size("seq")
    pairs = [(i, i + by) for i in range(length) if 0 <= i + by < length]
    return lax.ppermute(array, "seq", pairs)


def body(queries, key_heads, value_heads, output_grad, window, retrieved):
    tokens = queries.shape[0]
    per_device = tokens // BLOCK
    shards = lax.axis_size("seq")
    own_index = lax.axis_index("seq").astype(jnp.int32).reshape(1)
    wanted = exchange(wants_of(retrieved, shards))[:, 0, 0]

    kv = jnp.stack([key_heads, value_heads]).reshape(2, per_device, BLOCK, KVH, HD)
    kv = kv.transpose(3, 1, 0, 2, 4)
    prev = shifted(kv, 1)
    slot_hits = (wanted[:, None] == jnp.arange(per_device)[None, :]).astype(jnp.bfloat16)
    queries = pltpu.with_memory_space_constraint(queries.transpose(1, 0, 2), pltpu.HBM)
    output_grad = pltpu.with_memory_space_constraint(output_grad.transpose(1, 0, 2), pltpu.HBM)
    carried = ()
    fars = []
    replies = []
    returned = []
    for h in range(KVH):
        outgoing = jnp.take(kv[h], jnp.maximum(wanted, 0), axis=0, mode="clip")
        fars.append(exchange(outgoing))
    for h in range(KVH):
        *carried, dprev, dfar = attention_grads(
            h, own_index, window, retrieved, queries, output_grad, prev, kv, fars[h], *carried
        )
        replies.append(exchange(dfar))
        returned.append(shifted(dprev, -1).astype(jnp.float32))
    query_grad, down = carried
    sums = []
    for h in range(KVH):
        far_sum = jnp.einsum(
            "eb,e...->b...", slot_hits, replies[h], preferred_element_type=jnp.float32
        )
        sums.append(down[h] + returned[h] + far_sum)
    summed = jnp.stack(sums).transpose(2, 1, 3, 0, 4).astype(jnp.bfloat16)
    summed = summed.reshape(2, tokens, KVH, HD)
    return query_grad.transpose(1, 0, 2), summed[0], summed[1]


def solution(mesh):
    rows = P(("dp", "seq"), None, None)
    return jax.shard_map(
        body,
        mesh=mesh,
        in_specs=(rows, rows, rows, rows, P(("dp", "seq")), P(("dp", "seq"), None)),
        out_specs=(rows, rows, rows),
        check_vma=False,
    )
```

```python
import functools
import math

import jax
import jax.numpy as jnp
from jax import lax
from jax.experimental import pallas as pl
from jax.experimental.pallas import tpu as pltpu
from jax.sharding import PartitionSpec as P


HD = 128
QH = 14
KVH = 2
GROUP = QH // KVH
BLOCK = 128
SLAB = 32
MEMORY = 4
ROWS = GROUP * BLOCK
SCALE = HD ** (-0.5)
LOG2E = math.log2(math.e)

masked_score = -1e30


def contract(a, b, dims):
    return lax.dot_general(a, b, (dims, ((), ())), preferred_element_type=jnp.float32)


def fold(x, op):
    r = x[0:8]
    for k in range(1, x.shape[0] // 8):
        r = op(r, x[8 * k:8 * k + 8])
    return r


def list_near(per_device, b, own_ref, win_ref, slots):
    i = own_ref[0] * per_device + b
    earliest = i - win_ref[b]
    slots[0] = b + per_device
    count = jnp.int32(1)
    for back in range(1, per_device + 1):
        j = i - back
        slots[count] = b + per_device - back
        count = count + ((j >= 0) & (j > earliest)).astype(jnp.int32)
    return earliest, count


def list_far(per_device, b, ret_ref, earliest, count, slots):
    for r in range(MEMORY):
        e = ret_ref[b, r]
        live = e <= earliest
        for r2 in range(r):
            live = live & (e != ret_ref[b, r2])
        slots[count] = 2 * per_device + e // per_device
        count = count + live.astype(jnp.int32)
    return count


def kernel(per_device, shards, h, own_ref, win_ref, ret_ref, q_ref, g_ref, prev_ref, kv_ref, far_ref, *refs):
    if h > 0:
        refs = refs[2:]
    dq_ref, down_ref, dprev_ref, dfar_ref, kvs, acc, s_ref, dp_ref, dqt, slots = refs
    b = pl.program_id(0)
    near = 2 * per_device

    @pl.when(b == 0)
    def _():
        acc[...] = jnp.zeros_like(acc)
        kvs[0:per_device] = prev_ref[...]
        kvs[per_device:near] = kv_ref[0]
        kvs[near:near + shards] = far_ref[...]

    earliest, count = list_near(per_device, b, own_ref, win_ref, slots)
    count = list_far(per_device, b, ret_ref, earliest, count, slots)
    qh = q_ref.reshape(ROWS, HD)
    gh = g_ref.reshape(ROWS, HD)

    def each(body, first, stop, carry):
        for size in (4, 2, 1):
            whole = (stop - first) // size

            def wide(m, c, first=first, size=size):
                return body(first + m * size, size, c)

            carry = lax.fori_loop(0, whole, wide, carry)
            first = first + whole * size
        return carry

    def rows_at(n, width):
        return pl.ds(pl.multiple_of(n * BLOCK, BLOCK), width * BLOCK)

    def blocks(n, width, which):
        return jnp.concatenate([kvs[slots[n + k], which] for k in range(width)], axis=0)

    def products(n, width):
        dp_ref[rows_at(n, width), :] = contract(blocks(n, width, 1), gh[...], ((1,), (1,)))
        return contract(blocks(n, width, 0), qh[...], ((1,), (1,))) * (SCALE * LOG2E)

    key_pos = lax.broadcasted_iota(jnp.int32, (BLOCK, BLOCK), 0)
    query_pos = lax.broadcasted_iota(jnp.int32, (BLOCK, BLOCK), 1)
    above = jnp.where(key_pos <= query_pos, 0, 1)

    def score(n, width, top):
        s = products(n, width)
        hidden = above > n
        own = jnp.concatenate(
            [jnp.where(hidden, masked_score, s[:BLOCK, g * BLOCK:(g + 1) * BLOCK]) for g in range(GROUP)], axis=1)
        s = own if width == 1 else jnp.concatenate([own, s[BLOCK:]], axis=0)
        s_ref[rows_at(n, width), :] = s
        return jnp.maximum(top, fold(s, jnp.maximum))

    top = each(score, 0, count, jnp.full((8, ROWS), masked_score, jnp.float32))
    top = jnp.max(top, axis=0, keepdims=True)

    def slab(n, k):
        return pl.ds(pl.multiple_of(n * BLOCK, BLOCK) + k * SLAB, SLAB)

    def weigh_one(n, total):
        e = jnp.exp2(s_ref[rows_at(n, 1), :] - top)
        s_ref[rows_at(n, 1), :] = e
        return total + fold(e, jnp.add)

    total = lax.fori_loop(0, count, weigh_one, jnp.zeros((8, ROWS), jnp.float32))
    inverse = 1.0 / jnp.sum(total, axis=0, keepdims=True)

    def weigh_grad(n, delta):
        for k in range(BLOCK // SLAB):
            p = (s_ref[slab(n, k), :] * inverse).astype(jnp.bfloat16).astype(jnp.float32)
            delta = delta + fold(p * dp_ref[slab(n, k), :], jnp.add)
        return delta

    delta = lax.fori_loop(0, count, weigh_grad, jnp.zeros((8, ROWS), jnp.float32))
    delta = jnp.sum(delta, axis=0, keepdims=True)
    dqt[...] = jnp.zeros_like(dqt)

    def grads(n, width, carry):
        p = s_ref[rows_at(n, width), :] * inverse
        ds = (p * (dp_ref[rows_at(n, width), :] - delta)).astype(jnp.bfloat16)
        value_terms = contract(p.astype(jnp.bfloat16), gh[...], ((1,), (0,)))
        key_terms = contract(ds, qh[...], ((1,), (0,)))
        for k in range(width):
            c = slots[n + k]
            acc[c, 1] += value_terms[k * BLOCK:(k + 1) * BLOCK]
            acc[c, 0] += key_terms[k * BLOCK:(k + 1) * BLOCK]
        dqt[...] += contract(blocks(n, width, 0), ds, ((0,), (0,)))
        return carry

    each(grads, 0, count, 0)
    for g in range(GROUP):
        piece = (dqt[:, g * BLOCK:(g + 1) * BLOCK] * SCALE).astype(jnp.bfloat16)
        dq_ref[g] = piece.T

    @pl.when(b == per_device - 1)
    def _():
        for k in range(2):
            factor = SCALE if k == 0 else 1.0
            dprev_ref[:, k] = (acc[0:per_device, k] * factor).astype(jnp.bfloat16)
            down_ref[0, :, k] = acc[per_device:near, k] * factor
            dfar_ref[:, k] = (acc[near:near + shards, k] * factor).astype(jnp.bfloat16)


def attention_grads(h, own, window, retrieved, queries, output_grad, prev, kv, far, *carried):
    per_device = kv.shape[1]
    shards = far.shape[0]
    total = 2 * per_device + shards
    most = per_device + 1 + MEMORY
    pair = (2, BLOCK, HD)
    smem = pl.BlockSpec(memory_space=pltpu.SMEM)
    tokens = pl.BlockSpec((GROUP, BLOCK, HD), lambda b: (h, b, 0))
    of_head = pl.BlockSpec((1, per_device, *pair), lambda b: (h, 0, 0, 0, 0))
    of_owner = pl.BlockSpec((shards, *pair), lambda b: (0, 0, 0, 0))
    of_device = pl.BlockSpec((per_device, *pair), lambda b: (0, 0, 0, 0))
    return pl.pallas_call(
        functools.partial(kernel, per_device, shards, h),
        grid=(per_device,),
        in_specs=[smem, smem, smem, tokens, tokens, of_device, of_head, of_owner]
        + [pl.BlockSpec(memory_space=pl.ANY)] * len(carried),
        out_specs=[tokens, of_head, of_device, of_owner],
        out_shape=[
            pltpu.HBM(queries.shape, jnp.bfloat16),
            pltpu.HBM((KVH, per_device, *pair), jnp.float32),
            pltpu.HBM((per_device, *pair), jnp.bfloat16),
            pltpu.HBM((shards, *pair), jnp.bfloat16),
        ],
        scratch_shapes=[
            pltpu.VMEM((total, *pair), jnp.bfloat16),
            pltpu.VMEM((total, *pair), jnp.float32),
            pltpu.VMEM((most * BLOCK, ROWS), jnp.float32),
            pltpu.VMEM((most * BLOCK, ROWS), jnp.float32),
            pltpu.VMEM((HD, ROWS), jnp.float32),
            pltpu.SMEM((most + 1,), jnp.int32),
        ],
        input_output_aliases={8: 0, 9: 1} if carried else {},
        cost_estimate=pl.CostEstimate(
            flops=10 * per_device * most * BLOCK * ROWS * HD,
            transcendentals=per_device * most * BLOCK * ROWS,
            bytes_accessed=8 * queries.size,
        ),
        compiler_params=pltpu.CompilerParams(vmem_limit_bytes=36 << 20),
    )(own, window, retrieved, queries, output_grad, prev, kv, far, *carried)


def wants_kernel(per_device, ret_ref, out_ref):
    owners = lax.broadcasted_iota(jnp.int32, out_ref.shape, 0)
    wants = jnp.full(out_ref.shape, -1, jnp.int32)
    for b in range(per_device):
        for r in range(MEMORY):
            e = ret_ref[b, r]
            wants = jnp.where(owners == e // per_device, jnp.maximum(wants, e % per_device), wants)
    out_ref[...] = wants


def wants_of(retrieved, shards):
    return pl.pallas_call(
        functools.partial(wants_kernel, retrieved.shape[0]),
        in_specs=[pl.BlockSpec(memory_space=pltpu.SMEM)],
        out_shape=jax.ShapeDtypeStruct((shards, 8, HD), jnp.int32),
        name="wants",
    )(retrieved)


def pick_kernel(shards, wants_ref, kv_ref, out_ref):
    for d in range(shards):
        out_ref[d] = kv_ref[0, jnp.maximum(jnp.max(wants_ref[d]), 0)]


def pick(h, wants, kv):
    shards = wants.shape[0]
    return pl.pallas_call(
        functools.partial(pick_kernel, shards),
        grid=(1,),
        in_specs=[pl.BlockSpec(wants.shape, lambda i: (0, 0, 0)),
                  pl.BlockSpec((1, *kv.shape[1:]), lambda i: (h, 0, 0, 0, 0))],
        out_specs=pl.BlockSpec((shards, *kv.shape[2:]), lambda i: (0, 0, 0, 0)),
        out_shape=pltpu.HBM((shards, *kv.shape[2:]), kv.dtype),
        compiler_params=pltpu.CompilerParams(vmem_limit_bytes=16 << 20),
    )(wants, kv)


def exchange(array):
    return lax.all_to_all(array, "seq", split_axis=0, concat_axis=0, tiled=True)


def shifted(array, by):
    length = lax.axis_size("seq")
    pairs = [(i, i + by) for i in range(length) if 0 <= i + by < length]
    return lax.ppermute(array, "seq", pairs)


def body(queries, key_heads, value_heads, output_grad, window, retrieved):
    tokens = queries.shape[0]
    per_device = tokens // BLOCK
    shards = lax.axis_size("seq")
    own_index = lax.axis_index("seq").astype(jnp.int32).reshape(1)
    wants = exchange(wants_of(retrieved, shards))
    wanted = wants[:, 0, 0]

    kv = jnp.stack([key_heads, value_heads]).reshape(2, per_device, BLOCK, KVH, HD)
    kv = kv.transpose(3, 1, 0, 2, 4)
    prevs = [shifted(kv[h], 1) for h in range(KVH)]
    slot_hits = (wanted[:, None] == jnp.arange(per_device)[None, :]).astype(jnp.bfloat16)
    queries = pltpu.with_memory_space_constraint(queries.transpose(1, 0, 2), pltpu.HBM)
    output_grad = pltpu.with_memory_space_constraint(output_grad.transpose(1, 0, 2), pltpu.HBM)
    carried = ()
    fars = []
    replies = []
    returned = []
    for h in range(KVH):
        outgoing = pick(h, wants, kv)
        fars.append(exchange(outgoing))
    for h in range(KVH):
        *carried, dprev, dfar = attention_grads(
            h, own_index, window, retrieved, queries, output_grad, prevs[h], kv, fars[h], *carried
        )
        replies.append(exchange(dfar))
        returned.append(shifted(dprev, -1).astype(jnp.float32))
    query_grad, down = carried
    sums = []
    for h in range(KVH):
        far_sum = jnp.einsum(
            "eb,e...->b...", slot_hits, replies[h], preferred_element_type=jnp.float32
        )
        sums.append(down[h] + returned[h] + far_sum)
    summed = jnp.stack(sums).transpose(2, 1, 3, 0, 4).astype(jnp.bfloat16)
    summed = summed.reshape(2, tokens, KVH, HD)
    return query_grad.transpose(1, 0, 2), summed[0], summed[1]


def solution(mesh):
    rows = P(("dp", "seq"), None, None)
    return jax.shard_map(
        body,
        mesh=mesh,
        in_specs=(rows, rows, rows, rows, P(("dp", "seq")), P(("dp", "seq"), None)),
        out_specs=(rows, rows, rows),
        check_vma=False,
    )
```
